32 devices in a mesh: groups: 2 (over x), orient: 8 (over z, y), tile: 2 (over core).
Axes of the slice: x: 2, y: 2, z: 4, core: 2. Of those that a mesh axis runs over, the one named last changes fastest.
Arguments:
- spectra: float32 [16, 2, 256, 256], P(('groups', 'orient'), None, 'tile'), parts along dimension 0, may hold values from -6 to 6
- templates: float32 [8, 2, 256, 256], P('orient', None, 'tile'), may hold values from -1600 to 1600, as said below
- weights: float32 [512, 256], P('groups'), parts along dimension 0, may hold values from 0.1 to 1
Outputs:
- peak: float32 [16, 256, 256], P(('groups', 'orient'), 'tile'), parts along dimension 0
- mean_map: float32 [16, 256, 256], P(('groups', 'orient'), 'tile'), parts along dimension 0
- mean_square: float32 [16, 256, 256], P(('groups', 'orient'), 'tile'), parts along dimension 0
The draws below stay inside these ranges and needn't reach their ends.
There are 2 independent parts, one for each index of `groups`. The reference program is written for one: setup_inputs(seed, part) draws one part's arguments, and reference() takes and returns one part's arrays. A program takes and returns all parts, laid end to end along the dimension named above; an argument that names none is the same for every part. Nothing has to cross between parts.
Inputs may be any that keep to these rules, and one draw needn't show every extreme that they name: `templates`: finite real values.
All inputs are finite; a program needn't handle non-finite values.
Results may differ from the reference program's by a relative error of at most 0.00029.
Values sent between devices are 32-bit elements; how exact they have to be, the bound alone decides.
A program may use at most 64 MiB of HBM per device.

```python
import math
import jax
import jax.numpy as jnp
from jax import lax

L = 256
TILES = 8
ORIENTS = 8


def draw_templates(key, part):
    base_key = jax.random.fold_in(key, 11)
    row_key = jax.random.fold_in(key, 12)
    col_key = jax.random.fold_in(key, 13)
    shape = (ORIENTS, 2, L, L)
    base = jnp.clip(jax.random.normal(base_key, shape, jnp.float32), -6.0, 6.0)
    row_scale = jnp.exp(jax.random.uniform(row_key, (ORIENTS, 1, L, 1), jnp.float32, 0.0, 2.3))
    col_scale = jnp.exp(jax.random.uniform(col_key, (ORIENTS, 1, 1, L), jnp.float32, 0.0, 2.3))
    return base * row_scale * col_scale


def block_levels(key, extent, shards, smallest, high):
    def one(position, blocks):
        draws = jax.random.uniform(jax.random.fold_in(jax.random.fold_in(key, 6), position), (blocks,), jnp.float32, smallest / len(shards), high / len(shards))
        return jnp.repeat(jnp.exp(draws), extent[position] // blocks).reshape((-1,) + (1,) * (len(extent) - position - 1))

    level = one(*shards[0])
    for cut in shards[1:]:
        level = level * one(*cut)
    return level


def bell_draw(key, shape, deviation, most, split=(), held_as=jnp.bfloat16):
    entries = deviation * jax.random.normal(key, shape, jnp.float32)
    if split:
        entries = entries * block_levels(key, shape, split, -0.22, 0.18)
    return jnp.clip(entries, -most, most).astype(held_as)


def setup_inputs(seed: int = 0, part: int = 0) -> dict:
    streams_of = jax.random.split(jax.random.key(seed), 4)
    own_keys = jax.random.split(jax.random.fold_in(streams_of[3], part), 4)
    spectra = bell_draw(own_keys[0], (TILES, 2, L, L), 1.0, 6.0, ((0, 8), (2, 2)), jnp.float32)
    templates = draw_templates(jax.random.fold_in(streams_of[3], 71), part)
    weights = jnp.clip(jnp.exp(jax.random.uniform(own_keys[2], (L, L), jnp.float32, math.log(0.1), math.log(1.0))), 0.1, 1.0)
    return {"spectra": spectra, "templates": templates, "weights": weights}


def correlate(spectrum, normed_one, weights):
    real_part = (spectrum[0] * normed_one[0] + spectrum[1] * normed_one[1]) * weights
    imag_part = (spectrum[1] * normed_one[0] - spectrum[0] * normed_one[1]) * weights
    side = spectrum.shape[-1]
    return jnp.real(jnp.fft.ifft2(real_part + 1j * imag_part)) * side

def reference(spectra, templates, weights):
    power = lax.optimization_barrier(jnp.mean(templates * templates, axis=(1, 2, 3), keepdims=True))
    normed = templates / jnp.sqrt(power + 1e-06)

    def per_tile(spectrum):
        maps = lax.map(lambda one: correlate(spectrum, one, weights), normed)
        return (lax.optimization_barrier(jnp.max(maps, 0)), lax.optimization_barrier(jnp.mean(maps, 0)), lax.optimization_barrier(jnp.mean(maps * maps, 0)))
    peak, mean_map, mean_square = lax.map(per_tile, spectra)
    return (peak, mean_map, mean_square)
```

```python
import math

import jax
import jax.numpy as jnp
import ml_dtypes
import numpy as np
from jax import lax
from jax.experimental import pallas as pl
from jax.experimental.pallas import tpu as pltpu
from jax.sharding import PartitionSpec as P

MESH = pl.DeviceIdType.MESH
BF16 = jnp.bfloat16
F32 = jnp.float32


def two_parts(table):
    high = table.astype(np.float32).astype(ml_dtypes.bfloat16)
    low = (table - high.astype(np.float64)).astype(np.float32).astype(ml_dtypes.bfloat16)
    return np.stack([high, low])


def tables(side):
    freq = np.arange(side)
    angle = (freq[:, None] * freq[None, :] % side) * (2.0 * math.pi / side)
    cos, sin = np.cos(angle), np.sin(angle)
    rows = np.concatenate([np.concatenate([cos, -sin], 1), np.concatenate([-sin, -cos], 1)], 0)
    cols = np.concatenate([cos, sin], 0)
    return two_parts(rows), two_parts(cols)


def split(value):
    high = value.astype(BF16)
    return high, (value - high.astype(F32)).astype(BF16)


def dot(left, right):
    return jnp.dot(left, right, preferred_element_type=F32)


def correlator(side, count, pieces, white, z_parts, y_parts, row_ref, col_ref, stats):
    half = side // 2
    chunk = 64

    def one(template, first):
        square = jnp.zeros((8, side), F32)
        for at in range(0, side, chunk):
            h, row = at // half, at % half
            real = template.at[0, h][row : row + chunk]
            imag = template.at[1, h][row : row + chunk]
            s_real = white[0, at : at + chunk]
            s_imag = white[1, at : at + chunk]
            square = square + jnp.sum((real * real + imag * imag).reshape(chunk // 8, 8, side), 0)
            z_parts[0, at : at + chunk], z_parts[1, at : at + chunk] = split(s_real * real + s_imag * imag)
            below = slice(side + at, side + at + chunk)
            z_parts[0, below], z_parts[1, below] = split(s_imag * real - s_real * imag)
        power = jnp.sum(square, axis=(0, 1), keepdims=True) / (2.0 * side * side)
        factor = 1.0 / (jnp.sqrt(power + 1e-06) * side)
        for block in range(4):
            rows = slice(block * half, (block + 1) * half)
            part = dot(row_ref[0, rows], z_parts[0]) + dot(row_ref[0, rows], z_parts[1])
            part = part + dot(row_ref[1, rows], z_parts[0])
            to = slice((block % 2) * half, (block % 2 + 1) * half)
            lanes = slice((block // 2) * side, (block // 2 + 1) * side)
            y_parts[0, to, lanes], y_parts[1, to, lanes] = split(part)
        for block in range(2):
            rows = slice(block * half, (block + 1) * half)
            maps = dot(y_parts[0, rows], col_ref[0]) + dot(y_parts[1, rows], col_ref[0])
            maps = (maps + dot(y_parts[0, rows], col_ref[1])) * factor
            if first:
                stats[0, block] = maps
                stats[1, block] = maps
                stats[2, block] = maps * maps
            else:
                stats[0, block] = jnp.maximum(stats[0, block], maps)
                stats[1, block] += maps
                stats[2, block] += maps * maps

    return one


def kernel(side, count, spectra_ref, template_ref, weight_ref, row_ref, col_ref, peak_ref, mean_ref, square_ref,
           slots, spectrum, white, z_parts, y_parts, stats, other_stats,
           first_sem, pass_sem, piece_sem, spectrum_sem, stats_sem):
    half = side // 2
    x, orient, core = lax.axis_index("groups"), lax.axis_index("orient"), lax.axis_index("tile")
    y, z = orient % 2, orient // 2
    interior = jnp.logical_and(z > 0, z < 3)

    def chip(cx, cy, cz, c):
        return {"groups": cx, "orient": cz * 2 + cy, "tile": c}

    barrier = pltpu.get_barrier_semaphore()

    def greet(where):
        pl.semaphore_signal(barrier, inc=1, device_id=where, device_id_type=MESH)

    greet(chip(x, y, z, 1 - core))
    greet(chip(1 - x, y, z, core))
    for c in range(2):
        greet(chip(x, 1 - y, z, c))

    @pl.when(z > 0)
    def _():
        for c in range(2):
            greet(chip(x, y, z - 1, c))

    @pl.when(z < 3)
    def _():
        for c in range(2):
            greet(chip(x, y, z + 1, c))

    @pl.when(interior)
    def _():
        pl.semaphore_wait(barrier, 8)

    @pl.when(jnp.logical_not(interior))
    def _():
        pl.semaphore_wait(barrier, 6)

    home = (y + z) % 2

    def first_copy(p, way, where):
        return pltpu.make_async_remote_copy(
            src_ref=template_ref.at[0, p],
            dst_ref=slots.at[z, p, core],
            send_sem=first_sem.at[way, p],
            recv_sem=piece_sem.at[z, p, core],
            device_id=where,
            device_id_type=MESH,
        )

    def stay(p):
        return pltpu.make_async_copy(template_ref.at[0, p], slots.at[z, p, core], piece_sem.at[z, p, core])

    up, down = chip(x, y, z + 1, home), chip(x, y, z - 1, home)
    across, sibling = chip(x, 1 - y, z, home), chip(x, y, z, home)
    spectrum_copy = pltpu.make_async_remote_copy(
        src_ref=spectra_ref.at[0],
        dst_ref=spectrum,
        send_sem=spectrum_sem.at[0],
        recv_sem=spectrum_sem.at[1],
        device_id=chip(x, y, z, 1 - core),
        device_id_type=MESH,
    )
    for p in range(2):

        @pl.when(z < 3)
        def _():
            first_copy(p, 0, up).start()

        @pl.when(z > 0)
        def _():
            first_copy(p, 1, down).start()

        first_copy(p, 2, across).start()
    spectrum_copy.start()
    for p in range(2):

        @pl.when(home != core)
        def _():
            first_copy(p, 3, sibling).start()

        @pl.when(home == core)
        def _():
            stay(p).start()

    def arrived(s, p, h):
        ref = slots.at[s, p, h]
        pltpu.make_async_remote_copy(
            src_ref=ref, dst_ref=ref, send_sem=spectrum_sem.at[0], recv_sem=piece_sem.at[s, p, h],
            device_id=sibling, device_id_type=MESH,
        ).wait_recv()

    order = (z + 1 - 2 * (z % 2), 2 - z // 2, 3 - 3 * (z // 2))
    away = (3 - z, 3 * (z // 2), 3 * (z // 2))

    def pass_copy(k, p, way, where):
        ref = slots.at[order[k], p, x]
        return pltpu.make_async_remote_copy(
            src_ref=ref, dst_ref=ref, send_sem=pass_sem.at[k, p, way], recv_sem=piece_sem.at[order[k], p, x],
            device_id=where, device_id_type=MESH,
        )

    def passes(k, p):
        in_column = (core + order[k]) % 2 == y
        if k == 0:
            over = jnp.logical_not(in_column)
        elif k == 1:
            over = jnp.logical_not(jnp.logical_and(in_column, interior))
        else:
            over = None
        return (
            (jnp.logical_and(interior, in_column), pass_copy(k, p, 0, chip(x, y, away[k], core))),
            (in_column, pass_copy(k, p, 1, chip(x, 1 - y, z, core))),
            (over, pass_copy(k, p, 2, chip(1 - x, y, z, core))),
        )

    def hand_on(k):
        for p in range(2):
            arrived(order[k], p, x)
            for condition, copy in passes(k, p):
                if condition is None:
                    copy.start()
                else:
                    pl.when(condition)(copy.start)

    one = correlator(side, count, None, white, z_parts, y_parts, row_ref, col_ref, stats)

    spectrum_copy.wait_recv()
    for p in range(2):
        mine = pl.ds(pl.multiple_of(core * half, half), half)
        theirs = pl.ds(pl.multiple_of((1 - core) * half, half), half)
        white[p, mine] = spectra_ref[0, p] * weight_ref[mine]
        white[p, theirs] = spectrum[p] * weight_ref[theirs]

    hand_on(0)
    for p in range(2):
        for h in range(2):
            arrived(z, p, h)
    one(slots.at[z], True)
    hand_on(1)
    for k in range(3):
        for p in range(2):
            arrived(order[k], p, 1 - x)
        one(slots.at[order[k]], False)
        if k == 0:
            hand_on(2)

    stats_copy = [
        pltpu.make_async_remote_copy(
            src_ref=stats.at[i, 1 - core],
            dst_ref=other_stats.at[i],
            send_sem=stats_sem.at[0, i],
            recv_sem=stats_sem.at[1, i],
            device_id=chip(x, y, z, 1 - core),
            device_id_type=MESH,
        )
        for i in range(3)
    ]
    for copy in stats_copy:
        copy.start()
    stats_copy[0].wait_recv()
    peak_ref[0] = jnp.maximum(stats[0, core], other_stats[0])
    stats_copy[1].wait_recv()
    mean_ref[0] = (stats[1, core] + other_stats[1]) / count
    stats_copy[2].wait_recv()
    square_ref[0] = (stats[2, core] + other_stats[2]) / count

    for copy in stats_copy:
        copy.wait_send()
    spectrum_copy.wait_send()
    for p in range(2):

        @pl.when(z < 3)
        def _():
            first_copy(p, 0, up).wait_send()

        @pl.when(z > 0)
        def _():
            first_copy(p, 1, down).wait_send()

        first_copy(p, 2, across).wait_send()

        @pl.when(home != core)
        def _():
            first_copy(p, 3, sibling).wait_send()

        for k in range(3):
            for condition, copy in passes(k, p):
                if condition is None:
                    copy.wait_send()
                else:
                    pl.when(condition)(copy.wait_send)


def on_box(spectra, templates, weights):
    side, half = spectra.shape[3], spectra.shape[2]
    count = lax.axis_size("orient") * templates.shape[0]
    rows, cols = tables(side)
    out = jax.ShapeDtypeStruct((1, half, side), F32)

    def body(*refs):
        kernel(side, count, *refs)

    vmem = pl.BlockSpec(memory_space=pltpu.VMEM)
    return pl.pallas_call(
        body,
        out_shape=(out, out, out),
        in_specs=[vmem] * 5,
        out_specs=(vmem, vmem, vmem),
        scratch_shapes=[
            pltpu.VMEM((4, 2, 2, half, side), F32),
            pltpu.VMEM((2, half, side), F32),
            pltpu.VMEM((2, side, side), F32),
            pltpu.VMEM((2, 2 * side, side), BF16),
            pltpu.VMEM((2, side, 2 * side), BF16),
            pltpu.VMEM((3, 2, half, side), F32),
            pltpu.VMEM((3, half, side), F32),
            pltpu.SemaphoreType.DMA((4, 2)),
            pltpu.SemaphoreType.DMA((3, 2, 3)),
            pltpu.SemaphoreType.DMA((4, 2, 2)),
            pltpu.SemaphoreType.DMA((2,)),
            pltpu.SemaphoreType.DMA((2, 3)),
        ],
        compiler_params=pltpu.CompilerParams(
            collective_id=0, has_side_effects=True, vmem_limit_bytes=48 * 1024 * 1024
        ),
    )(spectra, templates, weights, jnp.asarray(rows), jnp.asarray(cols))


def twiddle(rows, cols, side):
    phase = rows[:, None] * cols[None, :] % side
    angle = phase.astype(F32) * (2.0 * math.pi / side)
    return (jnp.cos(angle), jnp.sin(angle))


def on_any(spectra, templates, weights):
    side, half = spectra.shape[3], spectra.shape[2]
    count = lax.axis_size("orient") * templates.shape[0]
    out_rows = lax.axis_index("tile") * half + lax.iota(jnp.int32, half)
    freq = lax.iota(jnp.int32, side)
    row_cos, row_sin = twiddle(out_rows, freq, side)
    col_cos, col_sin = twiddle(freq, freq, side)
    row_table = jnp.concatenate([row_cos, row_sin], 0)
    highest = lax.Precision.HIGHEST
    pieces = lax.all_gather(templates, ("orient",), axis=0, tiled=True)
    pieces = lax.all_gather(pieces, "tile", axis=2, tiled=True)
    full = lax.all_gather(spectra, "tile", axis=2, tiled=True)

    def one_orientation(carry, template):
        template = template / jnp.sqrt(jnp.mean(template * template) + 1e-06)
        real_part = (full[:, 0] * template[0] + full[:, 1] * template[1]) * weights
        imag_part = (full[:, 1] * template[0] - full[:, 0] * template[1]) * weights
        stack_real = jnp.einsum("yk,nkx->nyx", row_table, real_part, precision=highest)
        stack_imag = jnp.einsum("yk,nkx->nyx", row_table, imag_part, precision=highest)
        along_real = stack_real[:, :half] - stack_imag[:, half:]
        along_imag = stack_imag[:, :half] + stack_real[:, half:]
        maps = jnp.einsum("nyk,kx->nyx", along_real, col_cos, precision=highest)
        maps = (maps - jnp.einsum("nyk,kx->nyx", along_imag, col_sin, precision=highest)) / side
        best, total, squares = carry
        return ((jnp.maximum(best, maps), total + maps, squares + maps * maps), None)

    shape = (spectra.shape[0], half, side)
    initial = (jnp.full(shape, -jnp.inf, F32), jnp.zeros(shape, F32), jnp.zeros(shape, F32))
    (best, total, squares), _ = lax.scan(one_orientation, initial, pieces)
    return (best, total / count, squares / count)


def solution(mesh):
    box = dict(mesh.shape) == {"groups": 2, "orient": 8, "tile": 2}
    in_specs = (
        P(("groups", "orient"), None, "tile", None),
        P("orient", None, "tile", None),
        P("groups", None),
    )
    out_specs = (P(("groups", "orient"), "tile", None),) * 3
    body = on_box if box else on_any
    return jax.shard_map(body, mesh=mesh, in_specs=in_specs, out_specs=out_specs, check_vma=False)
```

```python
import math

import jax
import jax.numpy as jnp
import ml_dtypes
import numpy as np
from jax import lax
from jax.experimental import pallas as pl
from jax.experimental.pallas import tpu as pltpu
from jax.sharding import PartitionSpec as P

MESH = pl.DeviceIdType.MESH
BF16 = jnp.bfloat16
F32 = jnp.float32


def two_parts(table):
    high = table.astype(np.float32).astype(ml_dtypes.bfloat16)
    low = (table - high.astype(np.float64)).astype(np.float32).astype(ml_dtypes.bfloat16)
    return np.stack([high, low])


def tables(side):
    freq = np.arange(side)
    angle = (freq[:, None] * freq[None, :] % side) * (2.0 * math.pi / side)
    cos, sin = np.cos(angle), np.sin(angle)
    rows = np.concatenate([np.concatenate([cos, -sin], 1), np.concatenate([-sin, -cos], 1)], 0)
    cols = np.concatenate([cos, sin], 0)
    return two_parts(rows), two_parts(cols)


def split(value):
    high = value.astype(BF16)
    return high, (value - high.astype(F32)).astype(BF16)


def dot(left, right):
    return jnp.dot(left, right, preferred_element_type=F32)


def correlator(side, count, pieces, white, z_parts, y_parts, row_ref, col_ref, stats):
    half = side // 2
    chunk = half // 2

    def one(template, first):
        square = jnp.zeros((8, side), F32)
        for at in range(0, side, chunk):
            h, row = at // half, at % half
            real = template[0, h, row // chunk]
            imag = template[1, h, row // chunk]
            s_real = white[0, at : at + chunk]
            s_imag = white[1, at : at + chunk]
            square = square + jnp.sum((real * real + imag * imag).reshape(chunk // 8, 8, side), 0)
            z_parts[0, at : at + chunk], z_parts[1, at : at + chunk] = split(s_real * real + s_imag * imag)
            below = slice(side + at, side + at + chunk)
            z_parts[0, below], z_parts[1, below] = split(s_imag * real - s_real * imag)
        power = jnp.sum(square, axis=(0, 1), keepdims=True) / (2.0 * side * side)
        factor = 1.0 / (jnp.sqrt(power + 1e-06) * side)
        for block in range(4):
            rows = slice(block * half, (block + 1) * half)
            part = dot(row_ref[0, rows], z_parts[0]) + dot(row_ref[0, rows], z_parts[1])
            part = part + dot(row_ref[1, rows], z_parts[0])
            to = slice((block % 2) * half, (block % 2 + 1) * half)
            lanes = slice((block // 2) * side, (block // 2 + 1) * side)
            y_parts[0, to, lanes], y_parts[1, to, lanes] = split(part)
        for block in range(2):
            rows = slice(block * half, (block + 1) * half)
            maps = dot(y_parts[0, rows], col_ref[0]) + dot(y_parts[1, rows], col_ref[0])
            maps = (maps + dot(y_parts[0, rows], col_ref[1])) * factor
            if first:
                stats[0, block] = maps
                stats[1, block] = maps
                stats[2, block] = maps * maps
            else:
                stats[0, block] = jnp.maximum(stats[0, block], maps)
                stats[1, block] += maps
                stats[2, block] += maps * maps

    return one


def kernel(side, count, spectra_ref, template_ref, weight_ref, row_ref, col_ref, out_ref,
           slots, spectrum, weight, row_table, col_table, white, z_parts, y_parts, stats, other_stats,
           first_sem, pass_sem, piece_sem, spectrum_sem, stats_sem, load_sem):
    half = side // 2
    x, orient, core = lax.axis_index("groups"), lax.axis_index("orient"), lax.axis_index("tile")
    y, z = orient % 2, orient // 2
    interior = jnp.logical_and(z > 0, z < 3)

    def chip(cx, cy, cz, c):
        return {"groups": cx, "orient": cz * 2 + cy, "tile": c}

    loads = [
        pltpu.make_async_copy(spectra_ref.at[0], spectrum.at[core], load_sem.at[0]),
        pltpu.make_async_copy(weight_ref, weight, load_sem.at[1]),
        pltpu.make_async_copy(row_ref, row_table, load_sem.at[2]),
        pltpu.make_async_copy(col_ref, col_table, load_sem.at[3]),
    ]
    for copy in loads:
        copy.start()
    barrier = pltpu.get_barrier_semaphore()

    def greet(where):
        pl.semaphore_signal(barrier, inc=1, device_id=where, device_id_type=MESH)

    greet(chip(x, y, z, 1 - core))
    greet(chip(1 - x, y, z, core))
    for c in range(2):
        greet(chip(x, 1 - y, z, c))

    @pl.when(z > 0)
    def _():
        for c in range(2):
            greet(chip(x, y, z - 1, c))

    @pl.when(z < 3)
    def _():
        for c in range(2):
            greet(chip(x, y, z + 1, c))

    @pl.when(interior)
    def _():
        pl.semaphore_wait(barrier, 8)

    @pl.when(jnp.logical_not(interior))
    def _():
        pl.semaphore_wait(barrier, 6)

    home = (y + z) % 2

    fine = half // 2
    pieces = range(4)

    def first_copy(q, way, where):
        return pltpu.make_async_remote_copy(
            src_ref=template_ref.at[0, q // 2, pl.ds(q % 2 * fine, fine)],
            dst_ref=slots.at[z, q // 2, core, q % 2],
            send_sem=first_sem.at[way, q],
            recv_sem=piece_sem.at[z, core, q],
            device_id=where,
            device_id_type=MESH,
        )

    def stay(q):
        return pltpu.make_async_copy(
            template_ref.at[0, q // 2, pl.ds(q % 2 * fine, fine)],
            slots.at[z, q // 2, core, q % 2],
            piece_sem.at[z, core, q],
        )

    up, down, far = chip(x, y, z + 1, home), chip(x, y, z - 1, home), chip(x, y, 3 - z, home)
    across, sibling = chip(x, 1 - y, z, home), chip(x, y, z, home)
    chain = x == core

    def near(q, act):
        pl.when(z < 3)(lambda: act(first_copy(q, 0, up)))
        pl.when(z > 0)(lambda: act(first_copy(q, 1, down)))

    def along(act):
        for q in pieces:
            near(q, act)


    def start(copy):
        copy.start()

    def sent(copy):
        copy.wait_send()

    spectrum_copy = pltpu.make_async_remote_copy(
        src_ref=spectra_ref.at[0],
        dst_ref=spectrum.at[core],
        send_sem=spectrum_sem.at[0],
        recv_sem=spectrum_sem.at[1],
        device_id=chip(x, y, z, 1 - core),
        device_id_type=MESH,
    )
    for q in pieces:
        near(q, start)
        first_copy(q, 2, across).start()
    spectrum_copy.start()
    for q in pieces:
        pl.when(home != core)(first_copy(q, 3, sibling).start)
        pl.when(home == core)(stay(q).start)


    def arrived(s, h, q):
        ref = slots.at[s, q // 2, h, q % 2]
        pltpu.make_async_remote_copy(
            src_ref=ref, dst_ref=ref, send_sem=spectrum_sem.at[0], recv_sem=piece_sem.at[s, h, q],
            device_id=sibling, device_id_type=MESH,
        ).wait_recv()

    order = (z + 1 - 2 * (z % 2), 2 - z // 2, 3 - 3 * (z // 2))
    away = (3 - z, 3 * (z // 2), 3 * (z // 2))

    def pass_copy(k, q, way, where):
        ref = slots.at[order[k], q // 2, x, q % 2]
        return pltpu.make_async_remote_copy(
            src_ref=ref, dst_ref=ref, send_sem=pass_sem.at[k, q, way], recv_sem=piece_sem.at[order[k], x, q],
            device_id=where, device_id_type=MESH,
        )

    def passes(k, act, ready):
        in_column = (core + order[k]) % 2 == y
        outside = jnp.logical_not(in_column)
        over = (outside, jnp.logical_or(outside, jnp.logical_not(interior)), z >= 0)[k]
        for q in pieces:
            ready(q)
            if k < 3:
                pl.when(jnp.logical_and(interior, in_column))(
                    lambda: act(pass_copy(k, q, 0, chip(x, y, away[k], core)))
                )
            pl.when(in_column)(lambda: act(pass_copy(k, q, 1, chip(x, 1 - y, z, core))))
            pl.when(over)(lambda: act(pass_copy(k, q, 2, chip(1 - x, y, z, core))))

    def hand_on(k):
        passes(k, start, lambda q: arrived(order[k], x, q))

    one = correlator(side, count, None, white, z_parts, y_parts, row_table, col_table, stats)

    for copy in loads:
        copy.wait()
    spectrum_copy.wait_recv()
    for p in range(2):
        for h in range(2):
            rows = slice(h * half, (h + 1) * half)
            white[p, rows] = spectrum[h, p] * weight[rows]

    hand_on(0)
    hand_on(1)
    hand_on(2)
    for h in range(2):
        for q in pieces:
            arrived(z, h, q)
    one(slots.at[z], True)
    for k in range(3):
        for q in pieces:
            arrived(order[k], 1 - x, q)
        one(slots.at[order[k]], False)

    stats_copy = [
        pltpu.make_async_remote_copy(
            src_ref=stats.at[i, 1 - core],
            dst_ref=other_stats.at[i],
            send_sem=stats_sem.at[0, i],
            recv_sem=stats_sem.at[1, i],
            device_id=chip(x, y, z, 1 - core),
            device_id_type=MESH,
        )
        for i in range(3)
    ]
    for copy in stats_copy:
        copy.start()
    stats_copy[0].wait_recv()
    out_ref[0] = jnp.maximum(stats[0, core], other_stats[0])
    stats_copy[1].wait_recv()
    out_ref[1] = (stats[1, core] + other_stats[1]) / count
    stats_copy[2].wait_recv()
    out_ref[2] = (stats[2, core] + other_stats[2]) / count

    for copy in stats_copy:
        copy.wait_send()
    spectrum_copy.wait_send()
    along(sent)
    for q in pieces:
        first_copy(q, 2, across).wait_send()
        pl.when(home != core)(first_copy(q, 3, sibling).wait_send)
    for k in range(3):
        passes(k, sent, lambda q: None)


def on_box(spectra, templates, weights):
    side, half = spectra.shape[3], spectra.shape[2]
    count = lax.axis_size("orient") * templates.shape[0]
    rows, cols = tables(side)

    def body(*refs):
        kernel(side, count, *refs)

    vmem = pl.BlockSpec(memory_space=pltpu.VMEM)
    maps = pl.pallas_call(
        body,
        out_shape=jax.ShapeDtypeStruct((3, half, side), F32),
        in_specs=[pl.BlockSpec(memory_space=pl.ANY)] * 5,
        out_specs=vmem,
        scratch_shapes=[
            pltpu.VMEM((4, 2, 2, 2, half // 2, side), F32),
            pltpu.VMEM((2, 2, half, side), F32),
            pltpu.VMEM((side, side), F32),
            pltpu.VMEM((2, 2 * side, 2 * side), BF16),
            pltpu.VMEM((2, 2 * side, side), BF16),
            pltpu.VMEM((2, side, side), F32),
            pltpu.VMEM((2, 2 * side, side), BF16),
            pltpu.VMEM((2, side, 2 * side), BF16),
            pltpu.VMEM((3, 2, half, side), F32),
            pltpu.VMEM((3, half, side), F32),
            pltpu.SemaphoreType.DMA((5, 4)),
            pltpu.SemaphoreType.DMA((3, 4, 3)),
            pltpu.SemaphoreType.DMA((4, 2, 4)),
            pltpu.SemaphoreType.DMA((2,)),
            pltpu.SemaphoreType.DMA((2, 3)),
            pltpu.SemaphoreType.DMA((4,)),
        ],
        compiler_params=pltpu.CompilerParams(
            collective_id=0, has_side_effects=True, vmem_limit_bytes=60 * 1024 * 1024
        ),
    )(spectra, templates, weights, jnp.asarray(rows), jnp.asarray(cols))
    return (maps[0:1], maps[1:2], maps[2:3])


def twiddle(rows, cols, side):
    phase = rows[:, None] * cols[None, :] % side
    angle = phase.astype(F32) * (2.0 * math.pi / side)
    return (jnp.cos(angle), jnp.sin(angle))


def on_any(spectra, templates, weights):
    side, half = spectra.shape[3], spectra.shape[2]
    count = lax.axis_size("orient") * templates.shape[0]
    out_rows = lax.axis_index("tile") * half + lax.iota(jnp.int32, half)
    freq = lax.iota(jnp.int32, side)
    row_cos, row_sin = twiddle(out_rows, freq, side)
    col_cos, col_sin = twiddle(freq, freq, side)
    row_table = jnp.concatenate([row_cos, row_sin], 0)
    highest = lax.Precision.HIGHEST
    pieces = lax.all_gather(templates, ("orient",), axis=0, tiled=True)
    pieces = lax.all_gather(pieces, "tile", axis=2, tiled=True)
    full = lax.all_gather(spectra, "tile", axis=2, tiled=True)

    def one_orientation(carry, template):
        template = template / jnp.sqrt(jnp.mean(template * template) + 1e-06)
        real_part = (full[:, 0] * template[0] + full[:, 1] * template[1]) * weights
        imag_part = (full[:, 1] * template[0] - full[:, 0] * template[1]) * weights
        stack_real = jnp.einsum("yk,nkx->nyx", row_table, real_part, precision=highest)
        stack_imag = jnp.einsum("yk,nkx->nyx", row_table, imag_part, precision=highest)
        along_real = stack_real[:, :half] - stack_imag[:, half:]
        along_imag = stack_imag[:, :half] + stack_real[:, half:]
        maps = jnp.einsum("nyk,kx->nyx", along_real, col_cos, precision=highest)
        maps = (maps - jnp.einsum("nyk,kx->nyx", along_imag, col_sin, precision=highest)) / side
        best, total, squares = carry
        return ((jnp.maximum(best, maps), total + maps, squares + maps * maps), None)

    shape = (spectra.shape[0], half, side)
    initial = (jnp.full(shape, -jnp.inf, F32), jnp.zeros(shape, F32), jnp.zeros(shape, F32))
    (best, total, squares), _ = lax.scan(one_orientation, initial, pieces)
    return (best, total / count, squares / count)


def solution(mesh):
    box = dict(mesh.shape) == {"groups": 2, "orient": 8, "tile": 2}
    in_specs = (
        P(("groups", "orient"), None, "tile", None),
        P("orient", None, "tile", None),
        P("groups", None),
    )
    out_specs = (P(("groups", "orient"), "tile", None),) * 3
    body = on_box if box else on_any
    return jax.shard_map(body, mesh=mesh, in_specs=in_specs, out_specs=out_specs, check_vma=False)
```

```python
import math

import jax
import jax.numpy as jnp
import ml_dtypes
import numpy as np
from jax import lax
from jax.experimental import pallas as pl
from jax.experimental.pallas import tpu as pltpu
from jax.sharding import PartitionSpec as P

MESH = pl.DeviceIdType.MESH
BF16 = jnp.bfloat16
F32 = jnp.float32


def two_parts(table):
    high = table.astype(np.float32).astype(ml_dtypes.bfloat16)
    low = (table - high.astype(np.float64)).astype(np.float32).astype(ml_dtypes.bfloat16)
    return np.stack([high, low])


def tables(side):
    freq = np.arange(side)
    angle = (freq[:, None] * freq[None, :] % side) * (2.0 * math.pi / side)
    cos, sin = np.cos(angle), np.sin(angle)
    rows = np.concatenate([np.concatenate([cos, -sin], 1), np.concatenate([-sin, -cos], 1)], 0)
    cols = np.concatenate([cos, sin], 0)
    return two_parts(rows), two_parts(cols)


def split(value):
    high = value.astype(BF16)
    return high, (value - high.astype(F32)).astype(BF16)


def dot(left, right):
    return jnp.dot(left, right, preferred_element_type=F32)


def correlator(side, count, pieces, white, z_parts, y_parts, row_ref, col_ref, stats):
    half = side // 2
    chunk = half // 2

    def one(template, first):
        square = jnp.zeros((8, side), F32)
        for at in range(0, side, chunk):
            h, row = at // half, at % half
            real = template[0, h, row // chunk]
            imag = template[1, h, row // chunk]
            s_real = white[0, at : at + chunk]
            s_imag = white[1, at : at + chunk]
            square = square + jnp.sum((real * real + imag * imag).reshape(chunk // 8, 8, side), 0)
            z_parts[0, at : at + chunk], z_parts[1, at : at + chunk] = split(s_real * real + s_imag * imag)
            below = slice(side + at, side + at + chunk)
            z_parts[0, below], z_parts[1, below] = split(s_imag * real - s_real * imag)
        power = jnp.sum(square, axis=(0, 1), keepdims=True) / (2.0 * side * side)
        factor = 1.0 / (jnp.sqrt(power + 1e-06) * side)
        for block in range(4):
            rows = slice(block * half, (block + 1) * half)
            part = dot(row_ref[0, rows], z_parts[0]) + dot(row_ref[0, rows], z_parts[1])
            part = part + dot(row_ref[1, rows], z_parts[0])
            to = slice((block % 2) * half, (block % 2 + 1) * half)
            lanes = slice((block // 2) * side, (block // 2 + 1) * side)
            y_parts[0, to, lanes], y_parts[1, to, lanes] = split(part)
        for block in range(2):
            rows = slice(block * half, (block + 1) * half)
            maps = dot(y_parts[0, rows], col_ref[0]) + dot(y_parts[1, rows], col_ref[0])
            maps = (maps + dot(y_parts[0, rows], col_ref[1])) * factor
            if first:
                stats[0, block] = maps
                stats[1, block] = maps
                stats[2, block] = maps * maps
            else:
                stats[0, block] = jnp.maximum(stats[0, block], maps)
                stats[1, block] += maps
                stats[2, block] += maps * maps

    return one


def kernel(side, count, spectra_ref, template_ref, weight_ref, row_ref, col_ref, out_ref,
           slots, spectrum, weight, row_table, col_table, white, z_parts, y_parts, stats, other_stats,
           first_sem, pass_sem, piece_sem, spectrum_sem, stats_sem, load_sem):
    half = side // 2
    x, orient, core = lax.axis_index("groups"), lax.axis_index("orient"), lax.axis_index("tile")
    y, z = orient % 2, orient // 2
    interior = jnp.logical_and(z > 0, z < 3)

    def chip(cx, cy, cz, c):
        return {"groups": cx, "orient": cz * 2 + cy, "tile": c}

    loads = [
        pltpu.make_async_copy(spectra_ref.at[0], spectrum.at[core], load_sem.at[0]),
        pltpu.make_async_copy(weight_ref, weight, load_sem.at[1]),
        pltpu.make_async_copy(row_ref, row_table, load_sem.at[2]),
        pltpu.make_async_copy(col_ref, col_table, load_sem.at[3]),
    ]
    for copy in loads:
        copy.start()
    barrier = pltpu.get_barrier_semaphore()

    def greet(where):
        pl.semaphore_signal(barrier, inc=1, device_id=where, device_id_type=MESH)

    greet(chip(x, y, z, 1 - core))
    greet(chip(1 - x, y, z, core))
    for c in range(2):
        greet(chip(x, 1 - y, z, c))

    @pl.when(z > 0)
    def _():
        for c in range(2):
            greet(chip(x, y, z - 1, c))

    @pl.when(z < 3)
    def _():
        for c in range(2):
            greet(chip(x, y, z + 1, c))

    @pl.when(interior)
    def _():
        pl.semaphore_wait(barrier, 8)

    @pl.when(jnp.logical_not(interior))
    def _():
        pl.semaphore_wait(barrier, 6)

    home = (y + z) % 2

    fine = half // 2
    pieces = range(4)

    def first_copy(q, way, where):
        return pltpu.make_async_remote_copy(
            src_ref=template_ref.at[0, q // 2, pl.ds(q % 2 * fine, fine)],
            dst_ref=slots.at[z, q // 2, core, q % 2],
            send_sem=first_sem.at[way, q],
            recv_sem=piece_sem.at[z, core, q],
            device_id=where,
            device_id_type=MESH,
        )

    def stay(q):
        return pltpu.make_async_copy(
            template_ref.at[0, q // 2, pl.ds(q % 2 * fine, fine)],
            slots.at[z, q // 2, core, q % 2],
            piece_sem.at[z, core, q],
        )

    up, down = chip(x, y, z + 1, home), chip(x, y, z - 1, home)
    across, sibling = chip(x, 1 - y, z, home), chip(x, y, z, home)
    chain = x == core

    def near(q, act):
        pl.when(z < 3)(lambda: act(first_copy(q, 0, up)))
        pl.when(z > 0)(lambda: act(first_copy(q, 1, down)))

    def along(act):
        for q in pieces:
            near(q, act)

    def start(copy):
        copy.start()

    def sent(copy):
        copy.wait_send()

    spectrum_copy = pltpu.make_async_remote_copy(
        src_ref=spectra_ref.at[0],
        dst_ref=spectrum.at[core],
        send_sem=spectrum_sem.at[0],
        recv_sem=spectrum_sem.at[1],
        device_id=chip(x, y, z, 1 - core),
        device_id_type=MESH,
    )
    for q in pieces:
        pl.when(chain)(lambda: near(q, start))
        first_copy(q, 2, across).start()
    spectrum_copy.start()
    for q in pieces:
        pl.when(home != core)(first_copy(q, 3, sibling).start)
        pl.when(home == core)(stay(q).start)
    def arrived(s, h, q):
        ref = slots.at[s, q // 2, h, q % 2]
        pltpu.make_async_remote_copy(
            src_ref=ref, dst_ref=ref, send_sem=spectrum_sem.at[0], recv_sem=piece_sem.at[s, h, q],
            device_id=sibling, device_id_type=MESH,
        ).wait_recv()

    own = 1 - (z + core + y) % 2
    beside, across_z = z + 1 - 2 * (z % 2), (z + 2) % 4
    order = (
        own * across_z + (1 - own) * beside,
        own * beside + (1 - own) * (3 - z),
        own * (3 - z) + (1 - own) * across_z,
    )
    away = (own * 3 * (z // 2) + (1 - own) * (3 - z), 3 * (z // 2))

    def pass_copy(k, q, way, where):
        ref = slots.at[order[k], q // 2, x, q % 2]
        return pltpu.make_async_remote_copy(
            src_ref=ref, dst_ref=ref, send_sem=pass_sem.at[k, q, way], recv_sem=piece_sem.at[order[k], x, q],
            device_id=where, device_id_type=MESH,
        )

    def passes(k, act, ready):
        in_column = (z >= 0, own == 0, None)[k]
        over = z >= 0
        for q in pieces:
            ready(q)
            if k < 2:
                pl.when(jnp.logical_and(interior, in_column))(
                    lambda: act(pass_copy(k, q, 0, chip(x, y, away[k], core)))
                )
                pl.when(in_column)(lambda: act(pass_copy(k, q, 1, chip(x, 1 - y, z, core))))
            pl.when(over)(lambda: act(pass_copy(k, q, 2, chip(1 - x, y, z, core))))

    def hand_on(k):
        passes(k, start, lambda q: arrived(order[k], x, q))

    one = correlator(side, count, None, white, z_parts, y_parts, row_table, col_table, stats)

    for copy in loads:
        copy.wait()
    spectrum_copy.wait_recv()
    for p in range(2):
        for h in range(2):
            rows = slice(h * half, (h + 1) * half)
            white[p, rows] = spectrum[h, p] * weight[rows]

    hand_on(0)
    hand_on(1)
    hand_on(2)
    for h in range(2):
        for q in pieces:
            arrived(z, h, q)
    one(slots.at[z], True)
    for k in range(3):
        for q in pieces:
            arrived(order[k], 1 - x, q)
        one(slots.at[order[k]], False)

    stats_copy = [
        pltpu.make_async_remote_copy(
            src_ref=stats.at[i, 1 - core],
            dst_ref=other_stats.at[i],
            send_sem=stats_sem.at[0, i],
            recv_sem=stats_sem.at[1, i],
            device_id=chip(x, y, z, 1 - core),
            device_id_type=MESH,
        )
        for i in range(3)
    ]
    for copy in stats_copy:
        copy.start()
    stats_copy[0].wait_recv()
    out_ref[0] = jnp.maximum(stats[0, core], other_stats[0])
    stats_copy[1].wait_recv()
    out_ref[1] = (stats[1, core] + other_stats[1]) / count
    stats_copy[2].wait_recv()
    out_ref[2] = (stats[2, core] + other_stats[2]) / count

    for copy in stats_copy:
        copy.wait_send()
    spectrum_copy.wait_send()
    pl.when(chain)(lambda: along(sent))
    for q in pieces:
        first_copy(q, 2, across).wait_send()
        pl.when(home != core)(first_copy(q, 3, sibling).wait_send)
    for k in range(3):
        passes(k, sent, lambda q: None)


def on_box(spectra, templates, weights):
    side, half = spectra.shape[3], spectra.shape[2]
    count = lax.axis_size("orient") * templates.shape[0]
    rows, cols = tables(side)

    def body(*refs):
        kernel(side, count, *refs)

    vmem = pl.BlockSpec(memory_space=pltpu.VMEM)
    maps = pl.pallas_call(
        body,
        out_shape=jax.ShapeDtypeStruct((3, half, side), F32),
        in_specs=[pl.BlockSpec(memory_space=pl.ANY)] * 5,
        out_specs=vmem,
        scratch_shapes=[
            pltpu.VMEM((4, 2, 2, 2, half // 2, side), F32),
            pltpu.VMEM((2, 2, half, side), F32),
            pltpu.VMEM((side, side), F32),
            pltpu.VMEM((2, 2 * side, 2 * side), BF16),
            pltpu.VMEM((2, 2 * side, side), BF16),
            pltpu.VMEM((2, side, side), F32),
            pltpu.VMEM((2, 2 * side, side), BF16),
            pltpu.VMEM((2, side, 2 * side), BF16),
            pltpu.VMEM((3, 2, half, side), F32),
            pltpu.VMEM((3, half, side), F32),
            pltpu.SemaphoreType.DMA((5, 4)),
            pltpu.SemaphoreType.DMA((3, 4, 3)),
            pltpu.SemaphoreType.DMA((4, 2, 4)),
            pltpu.SemaphoreType.DMA((2,)),
            pltpu.SemaphoreType.DMA((2, 3)),
            pltpu.SemaphoreType.DMA((4,)),
        ],
        compiler_params=pltpu.CompilerParams(
            collective_id=0, has_side_effects=True, vmem_limit_bytes=60 * 1024 * 1024
        ),
    )(spectra, templates, weights, jnp.asarray(rows), jnp.asarray(cols))
    return (maps[0:1], maps[1:2], maps[2:3])


def twiddle(rows, cols, side):
    phase = rows[:, None] * cols[None, :] % side
    angle = phase.astype(F32) * (2.0 * math.pi / side)
    return (jnp.cos(angle), jnp.sin(angle))


def on_any(spectra, templates, weights):
    side, half = spectra.shape[3], spectra.shape[2]
    count = lax.axis_size("orient") * templates.shape[0]
    out_rows = lax.axis_index("tile") * half + lax.iota(jnp.int32, half)
    freq = lax.iota(jnp.int32, side)
    row_cos, row_sin = twiddle(out_rows, freq, side)
    col_cos, col_sin = twiddle(freq, freq, side)
    row_table = jnp.concatenate([row_cos, row_sin], 0)
    highest = lax.Precision.HIGHEST
    pieces = lax.all_gather(templates, ("orient",), axis=0, tiled=True)
    pieces = lax.all_gather(pieces, "tile", axis=2, tiled=True)
    full = lax.all_gather(spectra, "tile", axis=2, tiled=True)

    def one_orientation(carry, template):
        template = template / jnp.sqrt(jnp.mean(template * template) + 1e-06)
        real_part = (full[:, 0] * template[0] + full[:, 1] * template[1]) * weights
        imag_part = (full[:, 1] * template[0] - full[:, 0] * template[1]) * weights
        stack_real = jnp.einsum("yk,nkx->nyx", row_table, real_part, precision=highest)
        stack_imag = jnp.einsum("yk,nkx->nyx", row_table, imag_part, precision=highest)
        along_real = stack_real[:, :half] - stack_imag[:, half:]
        along_imag = stack_imag[:, :half] + stack_real[:, half:]
        maps = jnp.einsum("nyk,kx->nyx", along_real, col_cos, precision=highest)
        maps = (maps - jnp.einsum("nyk,kx->nyx", along_imag, col_sin, precision=highest)) / side
        best, total, squares = carry
        return ((jnp.maximum(best, maps), total + maps, squares + maps * maps), None)

    shape = (spectra.shape[0], half, side)
    initial = (jnp.full(shape, -jnp.inf, F32), jnp.zeros(shape, F32), jnp.zeros(shape, F32))
    (best, total, squares), _ = lax.scan(one_orientation, initial, pieces)
    return (best, total / count, squares / count)


def solution(mesh):
    box = dict(mesh.shape) == {"groups": 2, "orient": 8, "tile": 2}
    in_specs = (
        P(("groups", "orient"), None, "tile", None),
        P("orient", None, "tile", None),
        P("groups", None),
    )
    out_specs = (P(("groups", "orient"), "tile", None),) * 3
    body = on_box if box else on_any
    return jax.shard_map(body, mesh=mesh, in_specs=in_specs, out_specs=out_specs, check_vma=False)
```
